512 devices in a mesh: node: 16 (over y, core), cuts: 32 (over x, z).
Axes of the slice: x: 4, y: 8, z: 8, core: 2. Of those that a mesh axis runs over, the one named last changes fastest.
Arguments:
- transfer: float32 [16, 256, 256, 256], P('node', 'cuts'), may hold values from -0.09375 to 0.09375
- leaf_factors: float32 [16, 256, 256], P('node', 'cuts'), may hold values from -2 to 2, as said below
- node_of_slot: int32 [16], replicated, may hold values from 0 to 15, each once
Outputs:
- basis: float32 [16, 256, 256, 256], P('node', None, 'cuts')
- r_factor: float32 [16, 256, 256], P('node', 'cuts')
The draws below stay inside these ranges and needn't reach their ends.
Inputs may be any that keep to these rules, and one draw needn't show every extreme that they name: `leaf_factors`: each slice is upper triangular with its diagonal from 0.5 to 2.
All inputs are finite; a program needn't handle non-finite values.
Results may differ from the reference program's by a relative error of at most 0.0003.
Values sent between devices are 32-bit elements; how exact they have to be, the bound alone decides.
No kernel may reach another device: no remote copies, remote signals or barrier semaphores. Data moves between devices by JAX's collectives and lax.ppermute only.
A program may use at most 64 MiB of HBM per device.

```python
import math
import jax
import jax.numpy as jnp
from jax import lax

RANK = 256
SLOTS = 16


def draw_transfer(key, part):
    key_list = jax.random.split(key, 3)
    full_shape = (SLOTS, RANK, RANK, RANK)
    spread = 0.5 * math.log(10.0)
    column_scale = jnp.exp(jax.random.uniform(key_list[0], (SLOTS, RANK, 1, 1), jnp.float32, -spread, spread))
    position = jnp.arange(RANK, dtype=jnp.float32) / RANK - 0.5
    rising_scale = jnp.exp(position * math.log(3.0))[None, None, :, None]
    roughness = jnp.exp(jax.random.uniform(key_list[1], (SLOTS, 1, RANK, 1), jnp.float32, -0.35, 0.35))
    noise_part = jnp.clip(jax.random.normal(key_list[2], full_shape, jnp.float32), -4.0, 4.0)
    values = noise_part * column_scale * rising_scale * roughness / RANK
    return jnp.clip(values, -24.0 / RANK, 24.0 / RANK)


def draw_leaf_factors(key, part):
    key_list = jax.random.split(key, 2)
    diagonal = jnp.exp(jax.random.uniform(key_list[0], (SLOTS, RANK), jnp.float32, math.log(0.5), math.log(2.0)))
    off_diag = jnp.clip(jax.random.normal(key_list[1], (SLOTS, RANK, RANK), jnp.float32), -3.0, 3.0) * (0.5 / math.sqrt(RANK))
    upper_mask = jnp.arange(RANK)[:, None] < jnp.arange(RANK)[None, :]
    identity = jnp.eye(RANK, dtype=jnp.float32)[None]
    return jnp.where(upper_mask[None], off_diag, 0.0) + diagonal[:, :, None] * identity


def setup_inputs(seed: int = 0) -> dict:
    streams_of = jax.random.split(jax.random.key(seed), 4)
    return {
        "transfer": draw_transfer(jax.random.fold_in(streams_of[3], 71), 0),
        "leaf_factors": draw_leaf_factors(jax.random.fold_in(streams_of[3], 71), 0),
        "node_of_slot": jax.random.permutation(streams_of[2], SLOTS).astype(jnp.int32),
    }


HIGHEST = lax.Precision.HIGHEST

def contract_node(tensor, left_factor, right_factor):
    halfway = jnp.einsum('xa,pab->pxb', left_factor, tensor, precision=HIGHEST)
    return jnp.einsum('yb,pxb->pxy', right_factor, halfway, precision=HIGHEST)

def reference(transfer, leaf_factors, node_of_slot):
    slot_count = transfer.shape[0]
    rank_size = transfer.shape[1]
    slot_of = jnp.zeros((slot_count,), jnp.int32).at[node_of_slot].set(jnp.arange(slot_count, dtype=jnp.int32))
    factors = {}
    for leaf_index in range(slot_count):
        factors[slot_count + leaf_index] = leaf_factors[leaf_index]
    empty_tensor = jnp.zeros((rank_size, rank_size, rank_size), jnp.float32)
    empty_square = jnp.zeros((rank_size, rank_size), jnp.float32)
    basis_list = [empty_tensor] * slot_count
    uppers = [empty_square] * slot_count
    for node_index in range(slot_count - 1, 1, -1):
        tensor = transfer[slot_of[node_index]]
        mixed_tensor = contract_node(tensor, factors[2 * node_index], factors[2 * node_index + 1])
        flat_rows = mixed_tensor.reshape(rank_size, rank_size * rank_size)
        gram_matrix = jnp.dot(flat_rows.astype(jnp.float32), flat_rows.T.astype(jnp.float32), precision=HIGHEST, preferred_element_type=jnp.float32)
        lower_factor = jnp.linalg.cholesky(gram_matrix)
        upper_factor = lower_factor.T
        factors[node_index] = upper_factor
        solved = jax.scipy.linalg.solve_triangular(lower_factor, flat_rows, lower=True)
        basis_list[node_index] = (rank_size * solved).reshape(rank_size, rank_size, rank_size)
        uppers[node_index] = upper_factor
    basis_by_node = jnp.stack(basis_list)
    upper_by_node = jnp.stack(uppers)
    return (basis_by_node[node_of_slot], upper_by_node[node_of_slot])
```

```python
import functools

import jax
import jax.numpy as jnp
from jax import lax
from jax.experimental import pallas as pl
from jax.experimental.pallas import tpu as pltpu
from jax.sharding import PartitionSpec as P

HIGHEST = lax.Precision.HIGHEST
PANEL = 32
GROUP = 16


def from_everyone(array, axis):
    count = lax.axis_size(axis)
    return lax.all_to_all(
        jnp.broadcast_to(array[None], (count, *array.shape)), axis, 0, 0, tiled=True
    )


def eliminate(panel, first, columns):
    height, width = panel.shape
    lanes = 128
    row_ids = lax.broadcasted_iota(jnp.int32, (height, lanes), 0)
    for start in range(0, height, columns):
        copies = [
            jnp.broadcast_to(panel[:, first + start + i : first + start + i + 1], (height, lanes))
            for i in range(columns)
        ]
        for i in range(columns):
            pivot = start + i
            scaled = copies[i] * (1.0 / copies[i][pivot : pivot + 1, :])
            factor = jnp.where(row_ids > pivot, scaled, 0.0)
            for later in range(i + 1, columns):
                copies[later] = copies[later] - factor * copies[later][pivot : pivot + 1, :]
            wide = jnp.concatenate([factor] * (width // lanes), axis=1)
            panel = panel - wide * panel[pivot : pivot + 1, :]
    return panel


def cholesky_kernel(with_inverse, gram_ref, *refs):
    if with_inverse:
        upper_ref, inverse_ref, work_ref = refs
    else:
        upper_ref, work_ref = refs
    size = gram_ref.shape[0]
    for first in range(0, size, PANEL):
        rows = pl.ds(first, PANEL)
        panel = gram_ref[rows, :]
        row_ids = lax.broadcasted_iota(jnp.int32, (PANEL, size), 0) + first
        column_ids = lax.broadcasted_iota(jnp.int32, (PANEL, size), 1)
        if with_inverse:
            unit = (row_ids == column_ids).astype(jnp.float32)
            panel = jnp.concatenate([panel, unit], axis=1)
        if first:
            panel = panel - lax.dot_general(
                work_ref[0:first, first : first + PANEL],
                work_ref[0:first, :],
                (((0,), (0,)), ((), ())),
                precision=HIGHEST,
                preferred_element_type=jnp.float32,
            )
        panel = eliminate(panel, first, GROUP)
        square = panel[:, :size]
        pivots = jnp.sum(
            jnp.where(row_ids == column_ids, square, 0.0), axis=1, keepdims=True
        )
        panel = panel * lax.rsqrt(pivots)
        work_ref[rows, :] = panel
        upper_ref[rows, :] = jnp.where(column_ids >= row_ids, panel[:, :size], 0.0)
        if with_inverse:
            inverse_ref[rows, :] = panel[:, size:]


def upper_cholesky(gram, with_inverse=False):
    size = gram.shape[0]
    result = jax.ShapeDtypeStruct((size, size), jnp.float32)
    count = 2 if with_inverse else 1
    return pl.pallas_call(
        functools.partial(cholesky_kernel, with_inverse),
        out_shape=[result] * count,
        scratch_shapes=[pltpu.VMEM((size, count * size), jnp.float32)],
        cost_estimate=pl.CostEstimate(
            flops=20 * 10**9, bytes_accessed=2 * 4 * size * size, transcendentals=size
        ),
        name="upper_cholesky",
    )(gram)


def pick_children(rows_here, wanted):
    table = from_everyone(rows_here, "node")
    left = lax.dynamic_index_in_dim(table, wanted[0], 0, keepdims=False)
    right = lax.dynamic_index_in_dim(table, wanted[1], 0, keepdims=False)
    return jnp.stack([left, right])


def whole(rows):
    size = rows.shape[-1]
    gathered = from_everyone(rows, "cuts")
    return gathered[:, 0].reshape(-1, size), gathered[:, 1].reshape(-1, size)


def mix_left(tensor, left):
    halfway = jnp.einsum("xa,pab->pxb", left, tensor, precision=HIGHEST)
    return lax.all_to_all(halfway, "cuts", split_axis=1, concat_axis=0, tiled=True)


def gram_rows(mixed):
    size = mixed.shape[0]
    cut_count = lax.axis_size("cuts")
    partial = jnp.einsum("pxy,qxy->pq", mixed, mixed, precision=HIGHEST)
    pieces = lax.all_to_all(
        partial.reshape(cut_count, size // cut_count, size), "cuts", 0, 0, tiled=True
    )
    return jnp.sum(pieces, axis=0)


def mix_right(halfway, right):
    return jnp.einsum("yb,pxb->pxy", right, halfway, precision=HIGHEST)


def shards(transfer, leaf_factors, node_of_slot):
    slot_count = lax.axis_size("node")
    group_index = lax.axis_index("node")
    member_index = lax.axis_index("cuts")
    tensor = transfer[0]
    rank_size = tensor.shape[1]
    row_count = tensor.shape[0]
    slot_ids = lax.iota(jnp.int32, slot_count)
    node_id = node_of_slot[group_index]
    slot_of = jnp.sum(
        jnp.where(node_of_slot[None, :] == slot_ids[:, None], slot_ids[None, :], 0), axis=1
    )
    log_slots = slot_count.bit_length() - 1
    my_depth = jnp.zeros((), jnp.int32)
    for level_bit in range(1, log_slots):
        my_depth = my_depth + (node_id >= 2**level_bit).astype(jnp.int32)
    children = jnp.stack([2 * node_id, 2 * node_id + 1]) % slot_count

    left, right = whole(pick_children(leaf_factors[0], children))
    mixed = mix_right(mix_left(tensor, left), right)
    rows_here = gram_rows(mixed)

    def process(rows, tensor, mixed, rows_here):
        left_gram, right_gram = whole(rows)
        (left,) = upper_cholesky(left_gram)
        halfway = mix_left(tensor, left)
        (right,) = upper_cholesky(right_gram)
        mixed = mix_right(halfway, right)
        return mixed, gram_rows(mixed)

    def keep(rows, tensor, mixed, rows_here):
        return mixed, rows_here

    for level_now in range(log_slots - 2, 0, -1):
        rows = pick_children(rows_here, slot_of[children])
        mixed, rows_here = lax.cond(
            my_depth == level_now, process, keep, rows, tensor, mixed, rows_here
        )

    gram = from_everyone(rows_here, "cuts").reshape(rank_size, rank_size)
    upper, inverse = upper_cholesky(gram, with_inverse=True)
    active = my_depth > 0
    scaled = jnp.where(active, rank_size * inverse, 0.0)
    basis = jnp.einsum("qp,pxy->qxy", scaled, mixed, precision=HIGHEST)
    upper_rows = lax.dynamic_slice_in_dim(upper, member_index * row_count, row_count, 0)
    return basis[None], jnp.where(active, upper_rows, 0.0)[None]


def solution(mesh):
    placed = (P("node", "cuts", None, None), P("node", "cuts", None), P())
    return jax.shard_map(
        shards,
        mesh=mesh,
        in_specs=placed,
        out_specs=(P("node", None, "cuts", None), P("node", "cuts", None)),
        check_vma=False,
    )
```

```python
import functools

import jax
import jax.numpy as jnp
from jax import lax
from jax.experimental import pallas as pl
from jax.experimental.pallas import tpu as pltpu
from jax.sharding import PartitionSpec as P

HIGHEST = lax.Precision.HIGHEST
TILE = 8
LANES = 128
PANEL = 64
GROUP = 16
VMEM = pltpu.VMEM
PARAMS = pltpu.CompilerParams(vmem_limit_bytes=16 * 2**20)


def from_everyone(array, axis):
    count = lax.axis_size(axis)
    return lax.all_to_all(
        jnp.broadcast_to(array[None], (count, *array.shape)), axis, 0, 0, tiled=True
    )


def product(left, right, contracted):
    return lax.dot_general(
        left,
        right,
        ((contracted[:1], contracted[1:]), ((), ())),
        precision=HIGHEST,
        preferred_element_type=jnp.float32,
    )


def eliminate(tiles, first):
    count, width = len(tiles), tiles[0].shape[1]
    lines = lax.broadcasted_iota(jnp.int32, (TILE, LANES), 0)
    tiles = list(tiles)
    for start in range(0, count * TILE, GROUP):
        top = start // TILE
        copies = [
            [
                jnp.broadcast_to(tile[:, first + start + i : first + start + i + 1], (TILE, LANES))
                for tile in tiles[top:]
            ]
            for i in range(GROUP)
        ]
        for i in range(GROUP):
            home, line = divmod(start + i, TILE)
            low = home if line < TILE - 1 else home + 1
            inverse = 1.0 / copies[i][home - top][line : line + 1, :]
            factors = {}
            for t in range(low, count):
                factor = copies[i][t - top] * inverse
                factors[t] = jnp.where(lines > line, factor, 0.0) if t == home else factor
            for later in range(i + 1, GROUP):
                row = copies[later][home - top][line : line + 1, :]
                for t in range(low, count):
                    copies[later][t - top] = copies[later][t - top] - factors[t] * row
            row = tiles[home][line : line + 1, :]
            for t in range(low, count):
                wide = jnp.concatenate([factors[t]] * (width // LANES), axis=1)
                tiles[t] = tiles[t] - wide * row
    return tiles


def factor_gram(read_rows, size, work_ref, with_inverse=False):
    for first in range(0, size, PANEL):
        rows = pl.ds(first, PANEL)
        begin, end = first // LANES * LANES, size
        block = read_rows(first)[:, begin:]
        row_ids = lax.broadcasted_iota(jnp.int32, (PANEL, size), 0) + first
        column_ids = lax.broadcasted_iota(jnp.int32, (PANEL, size), 1)
        if with_inverse:
            reach = -(-(first + PANEL) // LANES) * LANES
            end = size + reach
            unit = (row_ids == column_ids).astype(jnp.float32)
            block = jnp.concatenate([block, unit[:, :reach]], axis=1)
        if first:
            block = block - product(
                work_ref[0:first, first : first + PANEL], work_ref[0:first, begin:end], (0, 0)
            )
        tiles = [block[t : t + TILE, :] for t in range(0, PANEL, TILE)]
        block = jnp.concatenate(eliminate(tiles, first - begin), axis=0)
        square = block[:, : size - begin]
        ahead = column_ids[:, begin:] - row_ids[:, begin:]
        pivots = jnp.sum(jnp.where(ahead == 0, square, 0.0), axis=1, keepdims=True)
        scale = lax.rsqrt(pivots)
        work_ref[rows, begin:size] = jnp.where(ahead >= 0, square * scale, 0.0)
        if begin:
            work_ref[rows, 0:begin] = jnp.zeros((PANEL, begin), jnp.float32)
        if with_inverse:
            work_ref[rows, size:end] = block[:, size - begin :] * scale
            if end < 2 * size:
                work_ref[rows, end:] = jnp.zeros((PANEL, 2 * size - end), jnp.float32)


def child_rows(gathered_ref, side):
    size = gathered_ref.shape[-1]

    def read_rows(first):
        members = pl.ds(first // TILE, PANEL // TILE)
        return gathered_ref[members, side].reshape(PANEL, size)

    return read_rows


def mix_tensor(left, tensor_ref, out_ref):
    count, size, _ = tensor_ref.shape
    for p in range(count):
        mixed = product(left, tensor_ref[p], (1, 0))
        for block in range(size // TILE):
            for half in range(size // LANES):
                out_ref[block, pl.ds(half * TILE * count + p, TILE, stride=count), :] = mixed[
                    block * TILE : (block + 1) * TILE, half * LANES : (half + 1) * LANES
                ]


def leaf_left_kernel(gathered_ref, tensor_ref, out_ref):
    size = tensor_ref.shape[1]
    mix_tensor(gathered_ref[:, 0].reshape(size, size), tensor_ref, out_ref)


def inner_left_kernel(gathered_ref, tensor_hbm, out_ref, tensor_ref, work_ref, done):
    size = tensor_ref.shape[1]
    copy = pltpu.make_async_copy(tensor_hbm, tensor_ref, done)
    copy.start()
    factor_gram(child_rows(gathered_ref, 0), size, work_ref)
    copy.wait()
    mix_tensor(work_ref[...], tensor_ref, out_ref)


def mix_left(gathered, tensor, inner):
    count, size, _ = tensor.shape
    result = jax.ShapeDtypeStruct((size // TILE, size * count // 16, LANES), jnp.float32)
    whole = pl.BlockSpec(memory_space=VMEM)
    mixed = pl.pallas_call(
        inner_left_kernel if inner else leaf_left_kernel,
        in_specs=[whole, pl.BlockSpec(memory_space=pl.ANY) if inner else whole],
        out_shape=result,
        scratch_shapes=[
            VMEM(tensor.shape, jnp.float32),
            VMEM((size, size), jnp.float32),
            pltpu.SemaphoreType.DMA(()),
        ]
        if inner
        else [],
        compiler_params=PARAMS,
        name="mix_left",
    )(gathered, tensor)
    return lax.all_to_all(mixed, "cuts", 0, 0, tiled=True)


def right_factor_kernel(gathered_ref, out_ref):
    size = out_ref.shape[0]
    factor_gram(child_rows(gathered_ref, 1), size, out_ref)


def right_factor(gathered):
    size = gathered.shape[-1]
    return pl.pallas_call(
        right_factor_kernel,
        out_shape=jax.ShapeDtypeStruct((size, size), jnp.float32),
        cost_estimate=pl.CostEstimate(
            flops=8 * 10**9, bytes_accessed=3 * 4 * size * size, transcendentals=size
        ),
        compiler_params=PARAMS,
        name="right_factor",
    )(gathered)


def mix_right_kernel(right_ref, halfway_ref, mixed_ref, gram_ref):
    size = gram_ref.shape[0]
    if len(right_ref.shape) == 4:
        right = right_ref[:, 1].reshape(size, size)
    else:
        right = right_ref[...]
    lines = mixed_ref.shape[0]
    parents = halfway_ref.shape[1] // (lines * (size // LANES))
    for x in range(lines):
        halves = []
        for half in range(size // LANES):
            rows = pl.ds((half * lines + x) * parents, parents)
            halves.append(halfway_ref[:, rows, :].reshape(size, LANES))
        mixed = product(jnp.concatenate(halves, axis=1), right, (1, 1))
        mixed_ref[x] = mixed
        term = product(mixed, mixed, (1, 1))
        gram_ref[...] = term if x == 0 else gram_ref[...] + term


def mix_right(halfway, right):
    size = right.shape[-1]
    mixed, partial = pl.pallas_call(
        mix_right_kernel,
        out_shape=[
            jax.ShapeDtypeStruct((TILE, size, size), jnp.float32),
            jax.ShapeDtypeStruct((size, size), jnp.float32),
        ],
        compiler_params=PARAMS,
        name="mix_right",
    )(right, halfway)
    cut_count = lax.axis_size("cuts")
    pieces = lax.all_to_all(
        partial.reshape(cut_count, size // cut_count, size), "cuts", 0, 0, tiled=True
    )
    return mixed, jnp.sum(pieces, axis=0)


def last_kernel(place_ref, gathered_ref, mixed_hbm, basis_ref, upper_ref, mixed_ref, work_ref, wide_ref, done):
    size = mixed_ref.shape[1]
    lines = mixed_ref.shape[0]
    copy = pltpu.make_async_copy(mixed_hbm, mixed_ref, done)
    copy.start()

    def read_rows(first):
        members = pl.ds(first // TILE, PANEL // TILE)
        return gathered_ref[members].reshape(PANEL, size)

    factor_gram(read_rows, size, work_ref, with_inverse=True)
    active = place_ref[1] > 0
    mine = pl.ds(pl.multiple_of(place_ref[0] * TILE, TILE), TILE)
    upper_ref[...] = jnp.where(active, work_ref[mine, 0:size], 0.0)
    inverse = jnp.where(active, work_ref[:, size:] * size, 0.0)
    copy.wait()
    for x in range(lines):
        solved = product(inverse, mixed_ref[x], (1, 0))
        for half in range(size // LANES):
            wide_ref[half, pl.ds(x, size, stride=lines), :] = solved[:, half * LANES : (half + 1) * LANES]
    for half in range(size // LANES):
        basis_ref[:, :, half * LANES : (half + 1) * LANES] = wide_ref[half].reshape(size, lines, LANES)


def last(place, gathered, mixed):
    lines, size, _ = mixed.shape
    whole = pl.BlockSpec(memory_space=VMEM)
    return pl.pallas_call(
        last_kernel,
        in_specs=[
            pl.BlockSpec(memory_space=pltpu.SMEM),
            whole,
            pl.BlockSpec(memory_space=pl.ANY),
        ],
        out_specs=[whole, whole],
        out_shape=[
            jax.ShapeDtypeStruct((size, lines, size), jnp.float32),
            jax.ShapeDtypeStruct((TILE, size), jnp.float32),
        ],
        scratch_shapes=[
            VMEM(mixed.shape, jnp.float32),
            VMEM((size, 2 * size), jnp.float32),
            VMEM((size // LANES, size * lines, LANES), jnp.float32),
            pltpu.SemaphoreType.DMA(()),
        ],
        compiler_params=PARAMS,
        name="last",
    )(place, gathered, mixed)


def pick_children(rows_here, chosen):
    table = from_everyone(rows_here, "node")
    picked = [jnp.sum(jnp.where(mask[:, None, None], table, 0.0), axis=0) for mask in chosen]
    return jnp.stack(picked)


def shards(transfer, leaf_factors, node_of_slot):
    slot_count = lax.axis_size("node")
    group_index = lax.axis_index("node")
    member_index = lax.axis_index("cuts")
    tensor = transfer[0]
    slot_ids = lax.iota(jnp.int32, slot_count)
    node_id = jnp.sum(jnp.where(slot_ids == group_index, node_of_slot, 0))
    log_slots = slot_count.bit_length() - 1
    my_depth = jnp.zeros((), jnp.int32)
    for level_bit in range(1, log_slots):
        my_depth = my_depth + (node_id >= 2**level_bit).astype(jnp.int32)
    children = [(2 * node_id + side) % slot_count for side in range(2)]
    place = jnp.stack([member_index.astype(jnp.int32), my_depth])

    rows = pick_children(leaf_factors[0], [slot_ids == child for child in children])
    gathered = from_everyone(rows, "cuts")
    halfway = mix_left(gathered, tensor, inner=False)
    mixed, rows_here = mix_right(halfway, gathered)

    def process(rows, tensor, mixed, rows_here):
        gathered = from_everyone(rows, "cuts")
        halfway = mix_left(gathered, tensor, inner=True)
        return mix_right(halfway, right_factor(gathered))

    def keep(rows, tensor, mixed, rows_here):
        return mixed, rows_here

    for level_now in range(log_slots - 2, 0, -1):
        rows = pick_children(rows_here, [node_of_slot == child for child in children])
        mixed, rows_here = lax.cond(
            my_depth == level_now, process, keep, rows, tensor, mixed, rows_here
        )

    gathered = from_everyone(rows_here, "cuts")
    basis, upper = last(place, gathered, mixed)
    return basis[None], upper[None]


def solution(mesh):
    placed = (P("node", "cuts", None, None), P("node", "cuts", None), P())
    return jax.shard_map(
        shards,
        mesh=mesh,
        in_specs=placed,
        out_specs=(P("node", None, "cuts", None), P("node", "cuts", None)),
        check_vma=False,
    )
```

```python
import functools

import jax
import jax.numpy as jnp
from jax import lax
from jax.experimental import pallas as pl
from jax.experimental.pallas import tpu as pltpu
from jax.sharding import PartitionSpec as P

HIGHEST = lax.Precision.HIGHEST
TILE = 8
LANES = 128
PANEL = 64
GROUP = 16
VMEM = pltpu.VMEM
PARAMS = pltpu.CompilerParams(vmem_limit_bytes=16 * 2**20)


def from_everyone(array, axis):
    count = lax.axis_size(axis)
    return lax.all_to_all(
        jnp.broadcast_to(array[None], (count, *array.shape)), axis, 0, 0, tiled=True
    )


def product(left, right, contracted):
    return lax.dot_general(
        left,
        right,
        ((contracted[:1], contracted[1:]), ((), ())),
        precision=HIGHEST,
        preferred_element_type=jnp.float32,
    )


def eliminate(tiles, first):
    count, width = len(tiles), tiles[0].shape[1]
    lines = lax.broadcasted_iota(jnp.int32, (TILE, LANES), 0)
    tiles = list(tiles)
    for start in range(0, count * TILE, GROUP):
        top = start // TILE
        copies = [
            [
                jnp.broadcast_to(tile[:, first + start + i : first + start + i + 1], (TILE, LANES))
                for tile in tiles[top:]
            ]
            for i in range(GROUP)
        ]
        for i in range(GROUP):
            home, line = divmod(start + i, TILE)
            low = home if line < TILE - 1 else home + 1
            inverse = 1.0 / copies[i][home - top][line : line + 1, :]
            factors = {}
            for t in range(low, count):
                factor = copies[i][t - top] * inverse
                factors[t] = jnp.where(lines > line, factor, 0.0) if t == home else factor
            for later in range(i + 1, GROUP):
                row = copies[later][home - top][line : line + 1, :]
                for t in range(low, count):
                    copies[later][t - top] = copies[later][t - top] - factors[t] * row
            row = tiles[home][line : line + 1, :]
            for t in range(low, count):
                wide = jnp.concatenate([factors[t]] * (width // LANES), axis=1)
                tiles[t] = tiles[t] - wide * row
    return tiles


def factor_gram(read_rows, size, work_ref, with_inverse=False):
    for first in range(0, size, PANEL):
        rows = pl.ds(first, PANEL)
        begin, end = first // LANES * LANES, size
        block = read_rows(first)[:, begin:]
        row_ids = lax.broadcasted_iota(jnp.int32, (PANEL, size), 0) + first
        column_ids = lax.broadcasted_iota(jnp.int32, (PANEL, size), 1)
        if with_inverse:
            reach = -(-(first + PANEL) // LANES) * LANES
            end = size + reach
            unit = (row_ids == column_ids).astype(jnp.float32)
            block = jnp.concatenate([block, unit[:, :reach]], axis=1)
        if first:
            block = block - product(
                work_ref[0:first, first : first + PANEL], work_ref[0:first, begin:end], (0, 0)
            )
        tiles = [block[t : t + TILE, :] for t in range(0, PANEL, TILE)]
        block = jnp.concatenate(eliminate(tiles, first - begin), axis=0)
        square = block[:, : size - begin]
        ahead = column_ids[:, begin:] - row_ids[:, begin:]
        pivots = jnp.sum(jnp.where(ahead == 0, square, 0.0), axis=1, keepdims=True)
        scale = lax.rsqrt(pivots)
        work_ref[rows, begin:size] = jnp.where(ahead >= 0, square * scale, 0.0)
        if begin:
            work_ref[rows, 0:begin] = jnp.zeros((PANEL, begin), jnp.float32)
        if with_inverse:
            work_ref[rows, size:end] = block[:, size - begin :] * scale
            if end < 2 * size:
                work_ref[rows, end:] = jnp.zeros((PANEL, 2 * size - end), jnp.float32)


def mix_tensor(left, tensor_ref, out_ref):
    count, size, _ = tensor_ref.shape
    for p in range(count):
        mixed = product(left, tensor_ref[p], (1, 0))
        for block in range(size // TILE):
            for half in range(size // LANES):
                out_ref[block, pl.ds(half * TILE * count + p, TILE, stride=count), :] = mixed[
                    block * TILE : (block + 1) * TILE, half * LANES : (half + 1) * LANES
                ]


def mix_left_kernel(left_ref, tensor_ref, out_ref):
    size = tensor_ref.shape[1]
    if len(left_ref.shape) == 4:
        left = left_ref[:, 0].reshape(size, size)
    else:
        left = left_ref[...]
    mix_tensor(left, tensor_ref, out_ref)


def mix_left(left, tensor):
    count, size, _ = tensor.shape
    blocks, half = size // TILE, size // LANES
    mixed = pl.pallas_call(
        mix_left_kernel,
        out_shape=jax.ShapeDtypeStruct((blocks, half * TILE * count, LANES), jnp.float32),
        compiler_params=PARAMS,
        name="mix_left",
    )(left, tensor)
    return lax.all_to_all(mixed, "cuts", 0, 0, tiled=True)


def child_factor_kernel(side_ref, gathered_ref, out_ref):
    size = out_ref.shape[0]
    side = side_ref[0]

    def read_rows(first):
        members = pl.ds(first // TILE, PANEL // TILE)
        return gathered_ref[members, side].reshape(PANEL, size)

    factor_gram(read_rows, size, out_ref)


def child_factor(gathered, side):
    size = gathered.shape[-1]
    whole = pl.BlockSpec(memory_space=VMEM)
    return pl.pallas_call(
        child_factor_kernel,
        in_specs=[pl.BlockSpec(memory_space=pltpu.SMEM), whole],
        out_shape=jax.ShapeDtypeStruct((size, size), jnp.float32),
        cost_estimate=pl.CostEstimate(
            flops=8 * 10**9, bytes_accessed=3 * 4 * size * size, transcendentals=size
        ),
        compiler_params=PARAMS,
        name="child_factor",
    )(jnp.full((1,), side, jnp.int32), gathered)


def mix_right_kernel(right_ref, halfway_ref, mixed_ref, gram_ref):
    size = gram_ref.shape[0]
    if len(right_ref.shape) == 4:
        right = right_ref[:, 1].reshape(size, size)
    else:
        right = right_ref[...]
    lines = mixed_ref.shape[0]
    parents = halfway_ref.shape[1] // (lines * (size // LANES))

    def add_line(x):
        halves = []
        for half in range(size // LANES):
            start = pl.multiple_of((half * lines + x) * parents, parents)
            halves.append(halfway_ref[:, pl.ds(start, parents), :].reshape(size, LANES))
        mixed = product(jnp.concatenate(halves, axis=1), right, (1, 1))
        mixed_ref[x] = mixed
        return product(mixed, mixed, (1, 1))

    gram_ref[...] = jnp.zeros_like(gram_ref)

    def add_lines(step, carry):
        gram_ref[...] += add_line(2 * step) + add_line(2 * step + 1)
        return carry

    lax.fori_loop(0, lines // 2, add_lines, 0)


def mix_right(halfway, right):
    size = right.shape[-1]
    mixed, partial = pl.pallas_call(
        mix_right_kernel,
        out_shape=[
            jax.ShapeDtypeStruct((TILE, size, size), jnp.float32),
            jax.ShapeDtypeStruct((size, size), jnp.float32),
        ],
        compiler_params=PARAMS,
        name="mix_right",
    )(right, halfway)
    cut_count = lax.axis_size("cuts")
    pieces = lax.all_to_all(
        partial.reshape(cut_count, size // cut_count, size), "cuts", 0, 0, tiled=True
    )
    return mixed, jnp.sum(pieces, axis=0)


def last_kernel(place_ref, gathered_ref, mixed_hbm, basis_ref, upper_ref, mixed_ref, work_ref, wide_ref, done):
    size = mixed_ref.shape[1]
    lines = mixed_ref.shape[0]
    copy = pltpu.make_async_copy(mixed_hbm, mixed_ref, done)
    copy.start()

    def read_rows(first):
        members = pl.ds(first // TILE, PANEL // TILE)
        return gathered_ref[members].reshape(PANEL, size)

    factor_gram(read_rows, size, work_ref, with_inverse=True)
    active = place_ref[1] > 0
    mine = pl.ds(pl.multiple_of(place_ref[0] * TILE, TILE), TILE)
    upper_ref[...] = jnp.where(active, work_ref[mine, 0:size], 0.0)
    inverse = jnp.where(active, work_ref[:, size:] * size, 0.0)
    copy.wait()
    for x in range(lines):
        solved = product(inverse, mixed_ref[x], (1, 0))
        for half in range(size // LANES):
            wide_ref[half, pl.ds(x, size, stride=lines), :] = solved[:, half * LANES : (half + 1) * LANES]
    for half in range(size // LANES):
        basis_ref[:, :, half * LANES : (half + 1) * LANES] = wide_ref[half].reshape(size, lines, LANES)


def last(place, gathered, mixed):
    lines, size, _ = mixed.shape
    whole = pl.BlockSpec(memory_space=VMEM)
    return pl.pallas_call(
        last_kernel,
        in_specs=[
            pl.BlockSpec(memory_space=pltpu.SMEM),
            whole,
            pl.BlockSpec(memory_space=pl.ANY),
        ],
        out_specs=[whole, whole],
        out_shape=[
            jax.ShapeDtypeStruct((size, lines, size), jnp.float32),
            jax.ShapeDtypeStruct((TILE, size), jnp.float32),
        ],
        scratch_shapes=[
            VMEM(mixed.shape, jnp.float32),
            VMEM((size, 2 * size), jnp.float32),
            VMEM((size // LANES, size * lines, LANES), jnp.float32),
            pltpu.SemaphoreType.DMA(()),
        ],
        compiler_params=PARAMS,
        name="last",
    )(place, gathered, mixed)


def pick_children(rows_here, chosen):
    table = from_everyone(rows_here, "node")
    picked = [jnp.sum(jnp.where(mask[:, None, None], table, 0.0), axis=0) for mask in chosen]
    return jnp.stack(picked)


def shards(transfer, leaf_factors, node_of_slot):
    slot_count = lax.axis_size("node")
    group_index = lax.axis_index("node")
    member_index = lax.axis_index("cuts")
    tensor = transfer[0]
    slot_ids = lax.iota(jnp.int32, slot_count)
    node_id = jnp.sum(jnp.where(slot_ids == group_index, node_of_slot, 0))
    log_slots = slot_count.bit_length() - 1
    my_depth = jnp.zeros((), jnp.int32)
    for level_bit in range(1, log_slots):
        my_depth = my_depth + (node_id >= 2**level_bit).astype(jnp.int32)
    children = [(2 * node_id + side) % slot_count for side in range(2)]
    place = jnp.stack([member_index.astype(jnp.int32), my_depth])

    rows = pick_children(leaf_factors[0], [slot_ids == child for child in children])
    gathered = from_everyone(rows, "cuts")
    halfway = mix_left(gathered, tensor)
    mixed, rows_here = mix_right(halfway, gathered)

    def process(rows, tensor, mixed, rows_here):
        gathered = from_everyone(rows, "cuts")
        halfway = mix_left(child_factor(gathered, 0), tensor)
        return mix_right(halfway, child_factor(gathered, 1))

    def keep(rows, tensor, mixed, rows_here):
        return mixed, rows_here

    def level(step, state):
        rows = pick_children(state[1], [node_of_slot == child for child in children])
        return lax.cond(my_depth == log_slots - 2 - step, process, keep, rows, tensor, *state)

    mixed, rows_here = lax.fori_loop(0, log_slots - 2, level, (mixed, rows_here))

    gathered = from_everyone(rows_here, "cuts")
    basis, upper = last(place, gathered, mixed)
    return basis[None], upper[None]


def solution(mesh):
    placed = (P("node", "cuts", None, None), P("node", "cuts", None), P())
    return jax.shard_map(
        shards,
        mesh=mesh,
        in_specs=placed,
        out_specs=(P("node", None, "cuts", None), P("node", "cuts", None)),
        check_vma=False,
    )
```

```python
import functools

import jax
import jax.numpy as jnp
from jax import lax
from jax.experimental import pallas as pl
from jax.experimental.pallas import tpu as pltpu
from jax.sharding import PartitionSpec as P

HIGHEST = lax.Precision.HIGHEST
TILE = 8
LANES = 128
PANEL = 64
GROUP = 16
VMEM = pltpu.VMEM
PARAMS = pltpu.CompilerParams(vmem_limit_bytes=16 * 2**20)


def from_everyone(array, axis):
    count = lax.axis_size(axis)
    return lax.all_to_all(
        jnp.broadcast_to(array[None], (count, *array.shape)), axis, 0, 0, tiled=True
    )


def product(left, right, contracted):
    return lax.dot_general(
        left,
        right,
        ((contracted[:1], contracted[1:]), ((), ())),
        precision=HIGHEST,
        preferred_element_type=jnp.float32,
    )


def eliminate(tiles, first):
    count, width = len(tiles), tiles[0].shape[1]
    lines = lax.broadcasted_iota(jnp.int32, (TILE, LANES), 0)
    tiles = list(tiles)
    for start in range(0, count * TILE, GROUP):
        top = start // TILE
        copies = [
            [
                jnp.broadcast_to(tile[:, first + start + i : first + start + i + 1], (TILE, LANES))
                for tile in tiles[top:]
            ]
            for i in range(GROUP)
        ]
        for i in range(GROUP):
            home, line = divmod(start + i, TILE)
            low = home if line < TILE - 1 else home + 1
            inverse = 1.0 / copies[i][home - top][line : line + 1, :]
            factors = {}
            for t in range(low, count):
                factor = copies[i][t - top] * inverse
                factors[t] = jnp.where(lines > line, factor, 0.0) if t == home else factor
            for later in range(i + 1, GROUP):
                row = copies[later][home - top][line : line + 1, :]
                for t in range(low, count):
                    copies[later][t - top] = copies[later][t - top] - factors[t] * row
            row = tiles[home][line : line + 1, :]
            for t in range(low, count):
                wide = jnp.concatenate([factors[t]] * (width // LANES), axis=1)
                tiles[t] = tiles[t] - wide * row
    return tiles


def factor_gram(read_rows, size, work_ref, with_inverse=False):
    for first in range(0, size, PANEL):
        rows = pl.ds(first, PANEL)
        begin, end = first // LANES * LANES, size
        block = read_rows(first)[:, begin:]
        row_ids = lax.broadcasted_iota(jnp.int32, (PANEL, size), 0) + first
        column_ids = lax.broadcasted_iota(jnp.int32, (PANEL, size), 1)
        if with_inverse:
            reach = -(-(first + PANEL) // LANES) * LANES
            end = size + reach
            unit = (row_ids == column_ids).astype(jnp.float32)
            block = jnp.concatenate([block, unit[:, :reach]], axis=1)
        if first:
            block = block - product(
                work_ref[0:first, first : first + PANEL], work_ref[0:first, begin:end], (0, 0)
            )
        tiles = [block[t : t + TILE, :] for t in range(0, PANEL, TILE)]
        block = jnp.concatenate(eliminate(tiles, first - begin), axis=0)
        square = block[:, : size - begin]
        ahead = column_ids[:, begin:] - row_ids[:, begin:]
        pivots = jnp.sum(jnp.where(ahead == 0, square, 0.0), axis=1, keepdims=True)
        scale = lax.rsqrt(pivots)
        work_ref[rows, begin:size] = jnp.where(ahead >= 0, square * scale, 0.0)
        if begin:
            work_ref[rows, 0:begin] = jnp.zeros((PANEL, begin), jnp.float32)
        if with_inverse:
            work_ref[rows, size:end] = block[:, size - begin :] * scale
            if end < 2 * size:
                work_ref[rows, end:] = jnp.zeros((PANEL, 2 * size - end), jnp.float32)


def mix_tensor(left, tensor_ref, out_ref):
    count, size, _ = tensor_ref.shape
    for p in range(count):
        mixed = product(left, tensor_ref[p], (1, 0))
        for block in range(size // TILE):
            for half in range(size // LANES):
                out_ref[block, pl.ds(half * TILE * count + p, TILE, stride=count), :] = mixed[
                    block * TILE : (block + 1) * TILE, half * LANES : (half + 1) * LANES
                ]


def child_matrix(leaf_ref, gathered_ref, side, out_ref):
    size = out_ref.shape[0]

    def read_rows(first):
        members = pl.ds(first // TILE, PANEL // TILE)
        return gathered_ref[members, side].reshape(PANEL, size)

    @pl.when(leaf_ref[0] > 0)
    def _():
        out_ref[...] = gathered_ref[:, side].reshape(size, size)

    @pl.when(leaf_ref[0] == 0)
    def _():
        factor_gram(read_rows, size, out_ref)


def mix_left_kernel(leaf_ref, gathered_ref, tensor_hbm, out_hbm, tensor_ref, left_ref, mixed_ref, load_sem, store_sems):
    load = pltpu.make_async_copy(tensor_hbm, tensor_ref, load_sem)
    load.start()
    child_matrix(leaf_ref, gathered_ref, 0, left_ref)
    load.wait()
    mix_tensor(left_ref[...], tensor_ref, mixed_ref)
    pieces = store_sems.shape[0]
    length = mixed_ref.shape[0] // pieces
    stores = []
    for i in range(pieces):
        part = pl.ds(i * length, length)
        stores.append(pltpu.make_async_copy(mixed_ref.at[part], out_hbm.at[part], store_sems.at[i]))
    for store in stores:
        store.start()
    for store in stores:
        store.wait()


def mix_left(leaf, gathered, tensor):
    count, size, _ = tensor.shape
    shape = (size // TILE, size // LANES * TILE * count, LANES)
    mixed = pl.pallas_call(
        mix_left_kernel,
        in_specs=[
            pl.BlockSpec(memory_space=pltpu.SMEM),
            pl.BlockSpec(memory_space=VMEM),
            pl.BlockSpec(memory_space=pl.ANY),
        ],
        out_specs=pl.BlockSpec(memory_space=pltpu.HBM),
        out_shape=jax.ShapeDtypeStruct(shape, jnp.float32),
        scratch_shapes=[
            VMEM(tensor.shape, jnp.float32),
            VMEM((size, size), jnp.float32),
            VMEM(shape, jnp.float32),
            pltpu.SemaphoreType.DMA(()),
            pltpu.SemaphoreType.DMA((4,)),
        ],
        compiler_params=pltpu.CompilerParams(vmem_limit_bytes=61_500_000),
        name="mix_left",
    )(leaf, gathered, tensor)
    return lax.all_to_all(mixed, "cuts", 0, 0, tiled=True)


def right_factor_kernel(leaf_ref, gathered_ref, out_ref):
    child_matrix(leaf_ref, gathered_ref, 1, out_ref)


def right_factor(leaf, gathered):
    size = gathered.shape[-1]
    return pl.pallas_call(
        right_factor_kernel,
        in_specs=[
            pl.BlockSpec(memory_space=pltpu.SMEM),
            pl.BlockSpec(memory_space=VMEM),
        ],
        out_shape=jax.ShapeDtypeStruct((size, size), jnp.float32),
        cost_estimate=pl.CostEstimate(
            flops=8 * 10**9, bytes_accessed=3 * 4 * size * size, transcendentals=size
        ),
        compiler_params=PARAMS,
        name="right_factor",
    )(leaf, gathered)


def mix_right_kernel(right_ref, halfway_ref, mixed_hbm, gram_ref, mixed_ref, store_sems):
    size = gram_ref.shape[0]
    right = right_ref[...]
    lines = mixed_ref.shape[0]
    parents = halfway_ref.shape[1] // (lines * (size // LANES))
    stores = []
    for x in range(lines):
        halves = []
        for half in range(size // LANES):
            rows = pl.ds((half * lines + x) * parents, parents)
            halves.append(halfway_ref[:, rows, :].reshape(size, LANES))
        mixed = product(jnp.concatenate(halves, axis=1), right, (1, 1))
        mixed_ref[x] = mixed
        stores.append(pltpu.make_async_copy(mixed_ref.at[x], mixed_hbm.at[x], store_sems.at[x]))
        stores[x].start()
        term = product(mixed, mixed, (1, 1))
        gram_ref[...] = term if x == 0 else gram_ref[...] + term
    for store in stores:
        store.wait()


def mix_right(halfway, right):
    size = right.shape[-1]
    mixed, partial = pl.pallas_call(
        mix_right_kernel,
        out_specs=[
            pl.BlockSpec(memory_space=pltpu.HBM),
            pl.BlockSpec(memory_space=VMEM),
        ],
        out_shape=[
            jax.ShapeDtypeStruct((TILE, size, size), jnp.float32),
            jax.ShapeDtypeStruct((size, size), jnp.float32),
        ],
        scratch_shapes=[
            VMEM((TILE, size, size), jnp.float32),
            pltpu.SemaphoreType.DMA((TILE,)),
        ],
        compiler_params=PARAMS,
        name="mix_right",
    )(right, halfway)
    cut_count = lax.axis_size("cuts")
    pieces = lax.all_to_all(
        partial.reshape(cut_count, size // cut_count, size), "cuts", 0, 0, tiled=True
    )
    return mixed, jnp.sum(pieces, axis=0)


def last_kernel(place_ref, gathered_ref, mixed_hbm, basis_ref, upper_ref, mixed_ref, work_ref, wide_ref, done):
    size = mixed_ref.shape[1]
    lines = mixed_ref.shape[0]
    copy = pltpu.make_async_copy(mixed_hbm, mixed_ref, done)
    copy.start()

    def read_rows(first):
        members = pl.ds(first // TILE, PANEL // TILE)
        return gathered_ref[members].reshape(PANEL, size)

    factor_gram(read_rows, size, work_ref, with_inverse=True)
    active = place_ref[1] > 0
    mine = pl.ds(pl.multiple_of(place_ref[0] * TILE, TILE), TILE)
    upper_ref[...] = jnp.where(active, work_ref[mine, 0:size], 0.0)
    inverse = jnp.where(active, work_ref[:, size:] * size, 0.0)
    copy.wait()
    for x in range(lines):
        solved = product(inverse, mixed_ref[x], (1, 0))
        for half in range(size // LANES):
            wide_ref[half, pl.ds(x, size, stride=lines), :] = solved[:, half * LANES : (half + 1) * LANES]
    for half in range(size // LANES):
        basis_ref[:, :, half * LANES : (half + 1) * LANES] = wide_ref[half].reshape(size, lines, LANES)


def last(place, gathered, mixed):
    lines, size, _ = mixed.shape
    whole = pl.BlockSpec(memory_space=VMEM)
    return pl.pallas_call(
        last_kernel,
        in_specs=[
            pl.BlockSpec(memory_space=pltpu.SMEM),
            whole,
            pl.BlockSpec(memory_space=pl.ANY),
        ],
        out_specs=[whole, whole],
        out_shape=[
            jax.ShapeDtypeStruct((size, lines, size), jnp.float32),
            jax.ShapeDtypeStruct((TILE, size), jnp.float32),
        ],
        scratch_shapes=[
            VMEM(mixed.shape, jnp.float32),
            VMEM((size, 2 * size), jnp.float32),
            VMEM((size // LANES, size * lines, LANES), jnp.float32),
            pltpu.SemaphoreType.DMA(()),
        ],
        compiler_params=PARAMS,
        name="last",
    )(place, gathered, mixed)


def pick_children(rows_here, chosen):
    table = from_everyone(rows_here, "node")
    picked = [jnp.sum(jnp.where(mask[:, None, None], table, 0.0), axis=0) for mask in chosen]
    return jnp.stack(picked)


def shards(transfer, leaf_factors, node_of_slot):
    slot_count = lax.axis_size("node")
    group_index = lax.axis_index("node")
    member_index = lax.axis_index("cuts")
    tensor = transfer[0]
    slot_ids = lax.iota(jnp.int32, slot_count)
    node_id = jnp.sum(jnp.where(slot_ids == group_index, node_of_slot, 0))
    log_slots = slot_count.bit_length() - 1
    my_depth = jnp.zeros((), jnp.int32)
    for level_bit in range(1, log_slots):
        my_depth = my_depth + (node_id >= 2**level_bit).astype(jnp.int32)
    children = [(2 * node_id + side) % slot_count for side in range(2)]
    place = jnp.stack([member_index.astype(jnp.int32), my_depth])

    def process(leaf, rows, mixed, rows_here):
        gathered = from_everyone(rows, "cuts")
        halfway = mix_left(leaf, gathered, tensor)
        return mix_right(halfway, right_factor(leaf, gathered))

    def keep(leaf, rows, mixed, rows_here):
        return mixed, rows_here

    def level(step, state):
        held = jnp.where(step == 0, slot_ids, node_of_slot)
        leaf = (step == 0).astype(jnp.int32).reshape(1)
        rows = pick_children(state[1], [held == child for child in children])
        return lax.cond(my_depth == log_slots - 1 - step, process, keep, leaf, rows, *state)

    state = (jnp.zeros_like(tensor), leaf_factors[0])
    mixed, rows_here = lax.fori_loop(0, log_slots - 1, level, state)

    gathered = from_everyone(rows_here, "cuts")
    basis, upper = last(place, gathered, mixed)
    return basis[None], upper[None]


def solution(mesh):
    placed = (P("node", "cuts", None, None), P("node", "cuts", None), P())
    return jax.shard_map(
        shards,
        mesh=mesh,
        in_specs=placed,
        out_specs=(P("node", None, "cuts", None), P("node", "cuts", None)),
        check_vma=False,
    )
```

```python
import functools

import jax
import jax.numpy as jnp
from jax import lax
from jax.experimental import pallas as pl
from jax.experimental.pallas import tpu as pltpu
from jax.sharding import PartitionSpec as P

HIGHEST = lax.Precision.HIGHEST
TILE = 8
LANES = 128
PANEL = 64
GROUP = 16
VMEM = pltpu.VMEM
PARAMS = pltpu.CompilerParams(vmem_limit_bytes=16 * 2**20)


def from_everyone(array, axis):
    count = lax.axis_size(axis)
    return lax.all_to_all(
        jnp.broadcast_to(array[None], (count, *array.shape)), axis, 0, 0, tiled=True
    )


def product(left, right, contracted):
    return lax.dot_general(
        left,
        right,
        ((contracted[:1], contracted[1:]), ((), ())),
        precision=HIGHEST,
        preferred_element_type=jnp.float32,
    )


def eliminate(tiles, first):
    count, width = len(tiles), tiles[0].shape[1]
    lines = lax.broadcasted_iota(jnp.int32, (TILE, LANES), 0)
    tiles = list(tiles)
    for start in range(0, count * TILE, GROUP):
        top = start // TILE
        copies = [
            [
                jnp.broadcast_to(tile[:, first + start + i : first + start + i + 1], (TILE, LANES))
                for tile in tiles[top:]
            ]
            for i in range(GROUP)
        ]
        for i in range(GROUP):
            home, line = divmod(start + i, TILE)
            low = home if line < TILE - 1 else home + 1
            inverse = 1.0 / copies[i][home - top][line : line + 1, :]
            factors = {}
            for t in range(low, count):
                factor = copies[i][t - top] * inverse
                factors[t] = jnp.where(lines > line, factor, 0.0) if t == home else factor
            for later in range(i + 1, GROUP):
                row = copies[later][home - top][line : line + 1, :]
                for t in range(low, count):
                    copies[later][t - top] = copies[later][t - top] - factors[t] * row
            row = tiles[home][line : line + 1, :]
            for t in range(low, count):
                wide = jnp.concatenate([factors[t]] * (width // LANES), axis=1)
                tiles[t] = tiles[t] - wide * row
    return tiles


def factor_gram(read_rows, size, work_ref, with_inverse=False):
    for first in range(0, size, PANEL):
        rows = pl.ds(first, PANEL)
        begin, end = first // LANES * LANES, size
        block = read_rows(first)[:, begin:]
        row_ids = lax.broadcasted_iota(jnp.int32, (PANEL, size), 0) + first
        column_ids = lax.broadcasted_iota(jnp.int32, (PANEL, size), 1)
        if with_inverse:
            reach = -(-(first + PANEL) // LANES) * LANES
            end = size + reach
            unit = (row_ids == column_ids).astype(jnp.float32)
            block = jnp.concatenate([block, unit[:, :reach]], axis=1)
        if first:
            block = block - product(
                work_ref[0:first, first : first + PANEL], work_ref[0:first, begin:end], (0, 0)
            )
        tiles = [block[t : t + TILE, :] for t in range(0, PANEL, TILE)]
        block = jnp.concatenate(eliminate(tiles, first - begin), axis=0)
        square = block[:, : size - begin]
        ahead = column_ids[:, begin:] - row_ids[:, begin:]
        pivots = jnp.sum(jnp.where(ahead == 0, square, 0.0), axis=1, keepdims=True)
        scale = lax.rsqrt(pivots)
        work_ref[rows, begin:size] = jnp.where(ahead >= 0, square * scale, 0.0)
        if begin:
            work_ref[rows, 0:begin] = jnp.zeros((PANEL, begin), jnp.float32)
        if with_inverse:
            work_ref[rows, size:end] = block[:, size - begin :] * scale
            if end < 2 * size:
                work_ref[rows, end:] = jnp.zeros((PANEL, 2 * size - end), jnp.float32)


def mix_tensor(left, tensor_ref, loads, out_ref):
    count, size, _ = tensor_ref.shape
    for p in range(count):
        loads[p].wait()
        mixed = product(left, tensor_ref[p], (1, 0))
        for block in range(size // TILE):
            for half in range(size // LANES):
                out_ref[block, pl.ds(half * TILE * count + p, TILE, stride=count), :] = mixed[
                    block * TILE : (block + 1) * TILE, half * LANES : (half + 1) * LANES
                ]


def child_matrix(leaf_ref, gathered_ref, side, out_ref):
    size = out_ref.shape[0]

    def read_rows(first):
        members = pl.ds(first // TILE, PANEL // TILE)
        return gathered_ref[members, side].reshape(PANEL, size)

    @pl.when(leaf_ref[0] > 0)
    def _():
        out_ref[...] = gathered_ref[:, side].reshape(size, size)

    @pl.when(leaf_ref[0] == 0)
    def _():
        factor_gram(read_rows, size, out_ref)


def mix_left_kernel(leaf_ref, gathered_ref, tensor_hbm, out_hbm, tensor_ref, left_ref, mixed_ref, load_sems, store_sems):
    loads = [
        pltpu.make_async_copy(tensor_hbm.at[p], tensor_ref.at[p], load_sems.at[p])
        for p in range(tensor_ref.shape[0])
    ]
    for load in loads:
        load.start()
    child_matrix(leaf_ref, gathered_ref, 0, left_ref)
    mix_tensor(left_ref[...], tensor_ref, loads, mixed_ref)
    pieces = store_sems.shape[0]
    length = mixed_ref.shape[0] // pieces
    stores = []
    for i in range(pieces):
        part = pl.ds(i * length, length)
        stores.append(pltpu.make_async_copy(mixed_ref.at[part], out_hbm.at[part], store_sems.at[i]))
    for store in stores:
        store.start()
    for store in stores:
        store.wait()


def mix_left(leaf, gathered, tensor):
    count, size, _ = tensor.shape
    shape = (size // TILE, size // LANES * TILE * count, LANES)
    mixed = pl.pallas_call(
        mix_left_kernel,
        in_specs=[
            pl.BlockSpec(memory_space=pltpu.SMEM),
            pl.BlockSpec(memory_space=VMEM),
            pl.BlockSpec(memory_space=pl.ANY),
        ],
        out_specs=pl.BlockSpec(memory_space=pltpu.HBM),
        out_shape=jax.ShapeDtypeStruct(shape, jnp.float32),
        scratch_shapes=[
            VMEM(tensor.shape, jnp.float32),
            VMEM((size, size), jnp.float32),
            VMEM(shape, jnp.float32),
            pltpu.SemaphoreType.DMA((count,)),
            pltpu.SemaphoreType.DMA((4,)),
        ],
        compiler_params=pltpu.CompilerParams(vmem_limit_bytes=61_000_000),
        name="mix_left",
    )(leaf, gathered, tensor)
    return lax.all_to_all(mixed, "cuts", 0, 0, tiled=True)


def right_factor_kernel(leaf_ref, gathered_ref, out_ref):
    child_matrix(leaf_ref, gathered_ref, 1, out_ref)


def right_factor(leaf, gathered):
    size = gathered.shape[-1]
    return pl.pallas_call(
        right_factor_kernel,
        in_specs=[
            pl.BlockSpec(memory_space=pltpu.SMEM),
            pl.BlockSpec(memory_space=VMEM),
        ],
        out_shape=jax.ShapeDtypeStruct((size, size), jnp.float32),
        cost_estimate=pl.CostEstimate(
            flops=8 * 10**9, bytes_accessed=3 * 4 * size * size, transcendentals=size
        ),
        compiler_params=PARAMS,
        name="right_factor",
    )(leaf, gathered)


def mix_right_kernel(right_ref, halfway_ref, mixed_hbm, gram_ref, mixed_ref, store_sems):
    size = gram_ref.shape[0]
    right = right_ref[...]
    lines = mixed_ref.shape[0]
    parents = halfway_ref.shape[1] // (lines * (size // LANES))
    stores = []
    for x in range(lines):
        halves = []
        for half in range(size // LANES):
            rows = pl.ds((half * lines + x) * parents, parents)
            halves.append(halfway_ref[:, rows, :].reshape(size, LANES))
        mixed = product(jnp.concatenate(halves, axis=1), right, (1, 1))
        mixed_ref[x] = mixed
        stores.append(pltpu.make_async_copy(mixed_ref.at[x], mixed_hbm.at[x], store_sems.at[x]))
        stores[x].start()
        term = product(mixed, mixed, (1, 1))
        gram_ref[...] = term if x == 0 else gram_ref[...] + term
    for store in stores:
        store.wait()


def mix_right(halfway, right):
    size = right.shape[-1]
    mixed, partial = pl.pallas_call(
        mix_right_kernel,
        out_specs=[
            pl.BlockSpec(memory_space=pltpu.HBM),
            pl.BlockSpec(memory_space=VMEM),
        ],
        out_shape=[
            jax.ShapeDtypeStruct((TILE, size, size), jnp.float32),
            jax.ShapeDtypeStruct((size, size), jnp.float32),
        ],
        scratch_shapes=[
            VMEM((TILE, size, size), jnp.float32),
            pltpu.SemaphoreType.DMA((TILE,)),
        ],
        compiler_params=PARAMS,
        name="mix_right",
    )(right, halfway)
    cut_count = lax.axis_size("cuts")
    pieces = lax.all_to_all(
        partial.reshape(cut_count, size // cut_count, size), "cuts", 0, 0, tiled=True
    )
    return mixed, jnp.sum(pieces, axis=0)


def last_kernel(place_ref, gathered_ref, mixed_hbm, basis_ref, upper_ref, mixed_ref, work_ref, wide_ref, done):
    size = mixed_ref.shape[1]
    lines = mixed_ref.shape[0]
    copy = pltpu.make_async_copy(mixed_hbm, mixed_ref, done)
    copy.start()

    def read_rows(first):
        members = pl.ds(first // TILE, PANEL // TILE)
        return gathered_ref[members].reshape(PANEL, size)

    factor_gram(read_rows, size, work_ref, with_inverse=True)
    active = place_ref[1] > 0
    mine = pl.ds(pl.multiple_of(place_ref[0] * TILE, TILE), TILE)
    upper_ref[...] = jnp.where(active, work_ref[mine, 0:size], 0.0)
    copy.wait()

    @pl.when(active)
    def _():
        inverse = work_ref[:, size:] * size
        for x in range(lines):
            solved = product(inverse, mixed_ref[x], (1, 0))
            for half in range(size // LANES):
                wide_ref[half, pl.ds(x, size, stride=lines), :] = solved[:, half * LANES : (half + 1) * LANES]
        for half in range(size // LANES):
            columns = pl.ds(half * LANES, LANES)
            basis_ref[:, :, columns] = wide_ref[half].reshape(size, lines, LANES)

    @pl.when(jnp.logical_not(active))
    def _():
        basis_ref[...] = jnp.zeros_like(basis_ref)


def last(place, gathered, mixed):
    lines, size, _ = mixed.shape
    whole = pl.BlockSpec(memory_space=VMEM)
    return pl.pallas_call(
        last_kernel,
        in_specs=[
            pl.BlockSpec(memory_space=pltpu.SMEM),
            whole,
            pl.BlockSpec(memory_space=pl.ANY),
        ],
        out_specs=[whole, whole],
        out_shape=[
            jax.ShapeDtypeStruct((size, lines, size), jnp.float32),
            jax.ShapeDtypeStruct((TILE, size), jnp.float32),
        ],
        scratch_shapes=[
            VMEM(mixed.shape, jnp.float32),
            VMEM((size, 2 * size), jnp.float32),
            VMEM((size // LANES, size * lines, LANES), jnp.float32),
            pltpu.SemaphoreType.DMA(()),
        ],
        compiler_params=PARAMS,
        name="last",
    )(place, gathered, mixed)


def unwritten(shape):
    return pl.pallas_call(
        lambda out_ref: None,
        out_specs=pl.BlockSpec(memory_space=pltpu.HBM),
        out_shape=jax.ShapeDtypeStruct(shape, jnp.float32),
        compiler_params=PARAMS,
        name="unwritten",
    )()


def pick_children(rows_here, held, children):
    chosen, rows_here = lax.optimization_barrier(
        ([held == child for child in children], rows_here)
    )
    table = from_everyone(rows_here, "node")
    picked = [jnp.sum(jnp.where(mask[:, None, None], table, 0.0), axis=0) for mask in chosen]
    return jnp.stack(picked)


def shards(transfer, leaf_factors, node_of_slot):
    slot_count = lax.axis_size("node")
    group_index = lax.axis_index("node")
    member_index = lax.axis_index("cuts")
    tensor = transfer[0]
    slot_ids = lax.iota(jnp.int32, slot_count)
    node_id = jnp.sum(jnp.where(slot_ids == group_index, node_of_slot, 0))
    log_slots = slot_count.bit_length() - 1
    my_depth = jnp.zeros((), jnp.int32)
    for level_bit in range(1, log_slots):
        my_depth = my_depth + (node_id >= 2**level_bit).astype(jnp.int32)
    children = [(2 * node_id + side) % slot_count for side in range(2)]
    place = jnp.stack([member_index.astype(jnp.int32), my_depth])

    def process(leaf, rows, mixed, rows_here):
        gathered = from_everyone(rows, "cuts")
        halfway = mix_left(leaf, gathered, tensor)
        return mix_right(halfway, right_factor(leaf, gathered))

    def keep(leaf, rows, mixed, rows_here):
        return mixed, rows_here

    def pick_inner(rows, rows_here):
        return pick_children(rows_here, node_of_slot, children)

    def level(step, state):
        rows, mixed, rows_here = state
        leaf = (step == 0).astype(jnp.int32).reshape(1)
        mixed, rows_here = lax.cond(
            my_depth == log_slots - 1 - step, process, keep, leaf, rows, mixed, rows_here
        )
        more = step < log_slots - 2
        rows = lax.cond(more, pick_inner, lambda rows, rows_here: rows, rows, rows_here)
        return rows, mixed, rows_here

    leaf_table = from_everyone(leaf_factors[0], "node")
    masks = [(slot_ids == child)[:, None, None] for child in children]
    rows = jnp.stack([jnp.sum(jnp.where(mask, leaf_table, 0.0), axis=0) for mask in masks])
    state = (rows, unwritten(tensor.shape), leaf_factors[0])
    _, mixed, rows_here = lax.fori_loop(0, log_slots - 1, level, state)
    place, rows_here = lax.optimization_barrier((place, rows_here))

    gathered = from_everyone(rows_here, "cuts")
    basis, upper = last(place, gathered, mixed)
    return basis[None], upper[None]


def solution(mesh):
    placed = (P("node", "cuts", None, None), P("node", "cuts", None), P())
    return jax.shard_map(
        shards,
        mesh=mesh,
        in_specs=placed,
        out_specs=(P("node", None, "cuts", None), P("node", "cuts", None)),
        check_vma=False,
    )
```

```python
import functools

import jax
import jax.numpy as jnp
from jax import lax
from jax.experimental import pallas as pl
from jax.experimental.pallas import tpu as pltpu
from jax.sharding import PartitionSpec as P

HIGHEST = lax.Precision.HIGHEST
TILE = 8
LANES = 128
PANEL = 64
GROUP = 16
VMEM = pltpu.VMEM
PARAMS = pltpu.CompilerParams(vmem_limit_bytes=16 * 2**20)


def from_everyone(array, axis):
    count = lax.axis_size(axis)
    return lax.all_to_all(
        jnp.broadcast_to(array[None], (count, *array.shape)), axis, 0, 0, tiled=True
    )


def product(left, right, contracted):
    return lax.dot_general(
        left,
        right,
        ((contracted[:1], contracted[1:]), ((), ())),
        precision=HIGHEST,
        preferred_element_type=jnp.float32,
    )


def eliminate(tiles, first):
    count, width = len(tiles), tiles[0].shape[1]
    lines = lax.broadcasted_iota(jnp.int32, (TILE, LANES), 0)
    tiles = list(tiles)
    for start in range(0, count * TILE, GROUP):
        top = start // TILE
        copies = [
            [
                jnp.broadcast_to(tile[:, first + start + i : first + start + i + 1], (TILE, LANES))
                for tile in tiles[top:]
            ]
            for i in range(GROUP)
        ]
        for i in range(GROUP):
            home, line = divmod(start + i, TILE)
            low = home if line < TILE - 1 else home + 1
            inverse = 1.0 / copies[i][home - top][line : line + 1, :]
            factors = {}
            for t in range(low, count):
                factor = copies[i][t - top] * inverse
                factors[t] = jnp.where(lines > line, factor, 0.0) if t == home else factor
            for later in range(i + 1, GROUP):
                row = copies[later][home - top][line : line + 1, :]
                for t in range(low, count):
                    copies[later][t - top] = copies[later][t - top] - factors[t] * row
            row = tiles[home][line : line + 1, :]
            for t in range(low, count):
                wide = jnp.concatenate([factors[t]] * (width // LANES), axis=1)
                tiles[t] = tiles[t] - wide * row
    return tiles


def factor_gram(read_rows, size, work_ref, with_inverse=False):
    for first in range(0, size, PANEL):
        rows = pl.ds(first, PANEL)
        begin, end = first // LANES * LANES, size
        block = read_rows(first)[:, begin:]
        row_ids = lax.broadcasted_iota(jnp.int32, (PANEL, size), 0) + first
        column_ids = lax.broadcasted_iota(jnp.int32, (PANEL, size), 1)
        if with_inverse:
            reach = -(-(first + PANEL) // LANES) * LANES
            end = size + reach
            unit = (row_ids == column_ids).astype(jnp.float32)
            block = jnp.concatenate([block, unit[:, :reach]], axis=1)
        if first:
            block = block - product(
                work_ref[0:first, first : first + PANEL], work_ref[0:first, begin:end], (0, 0)
            )
        tiles = [block[t : t + TILE, :] for t in range(0, PANEL, TILE)]
        block = jnp.concatenate(eliminate(tiles, first - begin), axis=0)
        square = block[:, : size - begin]
        ahead = column_ids[:, begin:] - row_ids[:, begin:]
        pivots = jnp.sum(jnp.where(ahead == 0, square, 0.0), axis=1, keepdims=True)
        scale = lax.rsqrt(pivots)
        work_ref[rows, begin:size] = jnp.where(ahead >= 0, square * scale, 0.0)
        if begin:
            work_ref[rows, 0:begin] = jnp.zeros((PANEL, begin), jnp.float32)
        if with_inverse:
            work_ref[rows, size:end] = block[:, size - begin :] * scale
            if end < 2 * size:
                work_ref[rows, end:] = jnp.zeros((PANEL, 2 * size - end), jnp.float32)


def mix_tensor(left, tensor_ref, out_ref):
    count, size, _ = tensor_ref.shape
    for p in range(count):
        mixed = product(left, tensor_ref[p], (1, 0))
        for block in range(size // TILE):
            for half in range(size // LANES):
                out_ref[block, pl.ds(half * TILE * count + p, TILE, stride=count), :] = mixed[
                    block * TILE : (block + 1) * TILE, half * LANES : (half + 1) * LANES
                ]


def child_matrix(leaf_ref, gathered_ref, side, out_ref):
    size = out_ref.shape[0]

    def read_rows(first):
        members = pl.ds(first // TILE, PANEL // TILE)
        return gathered_ref[members, side].reshape(PANEL, size)

    @pl.when(leaf_ref[0] > 0)
    def _():
        out_ref[...] = gathered_ref[:, side].reshape(size, size)

    @pl.when(leaf_ref[0] == 0)
    def _():
        factor_gram(read_rows, size, out_ref)


def mix_left_kernel(leaf_ref, gathered_ref, tensor_hbm, out_hbm, tensor_ref, left_ref, mixed_ref, load_sem, store_sems):
    load = pltpu.make_async_copy(tensor_hbm, tensor_ref, load_sem)
    load.start()
    child_matrix(leaf_ref, gathered_ref, 0, left_ref)
    load.wait()
    mix_tensor(left_ref[...], tensor_ref, mixed_ref)
    pieces = store_sems.shape[0]
    length = mixed_ref.shape[0] // pieces
    stores = []
    for i in range(pieces):
        part = pl.ds(i * length, length)
        stores.append(pltpu.make_async_copy(mixed_ref.at[part], out_hbm.at[part], store_sems.at[i]))
    for store in stores:
        store.start()
    for store in stores:
        store.wait()


def mix_left(leaf, gathered, tensor):
    count, size, _ = tensor.shape
    shape = (size // TILE, size // LANES * TILE * count, LANES)
    mixed = pl.pallas_call(
        mix_left_kernel,
        in_specs=[
            pl.BlockSpec(memory_space=pltpu.SMEM),
            pl.BlockSpec(memory_space=VMEM),
            pl.BlockSpec(memory_space=pl.ANY),
        ],
        out_specs=pl.BlockSpec(memory_space=pltpu.HBM),
        out_shape=jax.ShapeDtypeStruct(shape, jnp.float32),
        scratch_shapes=[
            VMEM(tensor.shape, jnp.float32),
            VMEM((size, size), jnp.float32),
            VMEM(shape, jnp.float32),
            pltpu.SemaphoreType.DMA(()),
            pltpu.SemaphoreType.DMA((4,)),
        ],
        compiler_params=pltpu.CompilerParams(vmem_limit_bytes=61_000_000),
        name="mix_left",
    )(leaf, gathered, tensor)
    return lax.all_to_all(mixed, "cuts", 0, 0, tiled=True)


def right_factor_kernel(leaf_ref, gathered_ref, out_ref):
    child_matrix(leaf_ref, gathered_ref, 1, out_ref)


def right_factor(leaf, gathered):
    size = gathered.shape[-1]
    return pl.pallas_call(
        right_factor_kernel,
        in_specs=[
            pl.BlockSpec(memory_space=pltpu.SMEM),
            pl.BlockSpec(memory_space=VMEM),
        ],
        out_shape=jax.ShapeDtypeStruct((size, size), jnp.float32),
        cost_estimate=pl.CostEstimate(
            flops=8 * 10**9, bytes_accessed=3 * 4 * size * size, transcendentals=size
        ),
        compiler_params=PARAMS,
        name="right_factor",
    )(leaf, gathered)


def mix_right_kernel(right_ref, halfway_ref, mixed_hbm, gram_ref, mixed_ref, store_sems):
    size = gram_ref.shape[0]
    right = right_ref[...]
    lines = mixed_ref.shape[0]
    parents = halfway_ref.shape[1] // (lines * (size // LANES))
    stores = []
    for x in range(lines):
        halves = []
        for half in range(size // LANES):
            rows = pl.ds((half * lines + x) * parents, parents)
            halves.append(halfway_ref[:, rows, :].reshape(size, LANES))
        mixed = product(jnp.concatenate(halves, axis=1), right, (1, 1))
        mixed_ref[x] = mixed
        stores.append(pltpu.make_async_copy(mixed_ref.at[x], mixed_hbm.at[x], store_sems.at[x]))
        stores[x].start()
        term = product(mixed, mixed, (1, 1))
        gram_ref[...] = term if x == 0 else gram_ref[...] + term
    for store in stores:
        store.wait()


def mix_right(halfway, right):
    size = right.shape[-1]
    mixed, partial = pl.pallas_call(
        mix_right_kernel,
        out_specs=[
            pl.BlockSpec(memory_space=pltpu.HBM),
            pl.BlockSpec(memory_space=VMEM),
        ],
        out_shape=[
            jax.ShapeDtypeStruct((TILE, size, size), jnp.float32),
            jax.ShapeDtypeStruct((size, size), jnp.float32),
        ],
        scratch_shapes=[
            VMEM((TILE, size, size), jnp.float32),
            pltpu.SemaphoreType.DMA((TILE,)),
        ],
        compiler_params=PARAMS,
        name="mix_right",
    )(right, halfway)
    cut_count = lax.axis_size("cuts")
    pieces = lax.all_to_all(
        partial.reshape(cut_count, size // cut_count, size), "cuts", 0, 0, tiled=True
    )
    return mixed, jnp.sum(pieces, axis=0)


def last_kernel(place_ref, gathered_ref, mixed_hbm, basis_ref, upper_ref, mixed_ref, work_ref, wide_ref, done):
    size = mixed_ref.shape[1]
    lines = mixed_ref.shape[0]
    copy = pltpu.make_async_copy(mixed_hbm, mixed_ref, done)
    copy.start()

    def read_rows(first):
        members = pl.ds(first // TILE, PANEL // TILE)
        return gathered_ref[members].reshape(PANEL, size)

    factor_gram(read_rows, size, work_ref, with_inverse=True)
    active = place_ref[1] > 0
    mine = pl.ds(pl.multiple_of(place_ref[0] * TILE, TILE), TILE)
    upper_ref[...] = jnp.where(active, work_ref[mine, 0:size], 0.0)
    copy.wait()

    @pl.when(active)
    def _():
        inverse = work_ref[:, size:] * size
        for x in range(lines):
            solved = product(inverse, mixed_ref[x], (1, 0))
            for half in range(size // LANES):
                wide_ref[half, pl.ds(x, size, stride=lines), :] = solved[:, half * LANES : (half + 1) * LANES]
        for half in range(size // LANES):
            columns = pl.ds(half * LANES, LANES)
            basis_ref[:, :, columns] = wide_ref[half].reshape(size, lines, LANES)

    @pl.when(jnp.logical_not(active))
    def _():
        basis_ref[...] = jnp.zeros_like(basis_ref)


def last(place, gathered, mixed):
    lines, size, _ = mixed.shape
    whole = pl.BlockSpec(memory_space=VMEM)
    return pl.pallas_call(
        last_kernel,
        in_specs=[
            pl.BlockSpec(memory_space=pltpu.SMEM),
            whole,
            pl.BlockSpec(memory_space=pl.ANY),
        ],
        out_specs=[whole, whole],
        out_shape=[
            jax.ShapeDtypeStruct((size, lines, size), jnp.float32),
            jax.ShapeDtypeStruct((TILE, size), jnp.float32),
        ],
        scratch_shapes=[
            VMEM(mixed.shape, jnp.float32),
            VMEM((size, 2 * size), jnp.float32),
            VMEM((size // LANES, size * lines, LANES), jnp.float32),
            pltpu.SemaphoreType.DMA(()),
        ],
        compiler_params=PARAMS,
        name="last",
    )(place, gathered, mixed)


def unwritten(shape):
    return pl.pallas_call(
        lambda out_ref: None,
        out_specs=pl.BlockSpec(memory_space=pltpu.HBM),
        out_shape=jax.ShapeDtypeStruct(shape, jnp.float32),
        compiler_params=PARAMS,
        name="unwritten",
    )()


def pick_children(rows_here, held, children):
    chosen, rows_here = lax.optimization_barrier(
        ([held == child for child in children], rows_here)
    )
    table = from_everyone(rows_here, "node")
    picked = [jnp.sum(jnp.where(mask[:, None, None], table, 0.0), axis=0) for mask in chosen]
    return jnp.stack(picked)


def shards(transfer, leaf_factors, node_of_slot):
    slot_count = lax.axis_size("node")
    group_index = lax.axis_index("node")
    member_index = lax.axis_index("cuts")
    tensor = transfer[0]
    slot_ids = lax.iota(jnp.int32, slot_count)
    node_id = jnp.sum(jnp.where(slot_ids == group_index, node_of_slot, 0))
    log_slots = slot_count.bit_length() - 1
    my_depth = jnp.zeros((), jnp.int32)
    for level_bit in range(1, log_slots):
        my_depth = my_depth + (node_id >= 2**level_bit).astype(jnp.int32)
    children = [(2 * node_id + side) % slot_count for side in range(2)]
    place = jnp.stack([member_index.astype(jnp.int32), my_depth])

    def process(leaf, rows, mixed, rows_here):
        gathered = from_everyone(rows, "cuts")
        halfway = mix_left(leaf, gathered, tensor)
        return mix_right(halfway, right_factor(leaf, gathered))

    def keep(leaf, rows, mixed, rows_here):
        return mixed, rows_here

    def pick_inner(rows, rows_here):
        return pick_children(rows_here, node_of_slot, children)

    def level(step, state):
        rows, mixed, rows_here = state
        leaf = (step == 0).astype(jnp.int32).reshape(1)
        mixed, rows_here = lax.cond(
            my_depth == log_slots - 1 - step, process, keep, leaf, rows, mixed, rows_here
        )
        more = step < log_slots - 2
        rows = lax.cond(more, pick_inner, lambda rows, rows_here: rows, rows, rows_here)
        return rows, mixed, rows_here

    leaf_table = from_everyone(leaf_factors[0], "node")
    masks = [(slot_ids == child)[:, None, None] for child in children]
    rows = jnp.stack([jnp.sum(jnp.where(mask, leaf_table, 0.0), axis=0) for mask in masks])
    state = (rows, unwritten(tensor.shape), leaf_factors[0])
    _, mixed, rows_here = lax.fori_loop(0, log_slots - 1, level, state)
    place, rows_here = lax.optimization_barrier((place, rows_here))

    gathered = from_everyone(rows_here, "cuts")
    basis, upper = last(place, gathered, mixed)
    return basis[None], upper[None]


def solution(mesh):
    placed = (P("node", "cuts", None, None), P("node", "cuts", None), P())
    return jax.shard_map(
        shards,
        mesh=mesh,
        in_specs=placed,
        out_specs=(P("node", None, "cuts", None), P("node", "cuts", None)),
        check_vma=False,
    )
```

```python
import functools

import jax
import jax.numpy as jnp
from jax import lax
from jax.experimental import pallas as pl
from jax.experimental.pallas import tpu as pltpu
from jax.sharding import PartitionSpec as P

HIGHEST = lax.Precision.HIGHEST
TILE = 8
LANES = 128
PANEL = 64
GROUP = 16
VMEM = pltpu.VMEM
PARAMS = pltpu.CompilerParams(vmem_limit_bytes=16 * 2**20)


def from_everyone(array, axis):
    count = lax.axis_size(axis)
    return lax.all_to_all(
        jnp.broadcast_to(array[None], (count, *array.shape)), axis, 0, 0, tiled=True
    )


def product(left, right, contracted):
    return lax.dot_general(
        left,
        right,
        ((contracted[:1], contracted[1:]), ((), ())),
        precision=HIGHEST,
        preferred_element_type=jnp.float32,
    )


def eliminate(tiles, first):
    count, width = len(tiles), tiles[0].shape[1]
    lines = lax.broadcasted_iota(jnp.int32, (TILE, LANES), 0)
    tiles = list(tiles)
    for start in range(0, count * TILE, GROUP):
        top = start // TILE
        copies = [
            [
                jnp.broadcast_to(tile[:, first + start + i : first + start + i + 1], (TILE, LANES))
                for tile in tiles[top:]
            ]
            for i in range(GROUP)
        ]
        for i in range(GROUP):
            home, line = divmod(start + i, TILE)
            low = home if line < TILE - 1 else home + 1
            scale = lax.rsqrt(copies[i][home - top][line : line + 1, :])
            factors = {}
            for t in range(low, count):
                factor = copies[i][t - top] * scale
                factors[t] = jnp.where(lines > line, factor, 0.0) if t == home else factor
            for later in range(i + 1, GROUP):
                row = copies[later][home - top][line : line + 1, :] * scale
                for t in range(low, count):
                    copies[later][t - top] = copies[later][t - top] - factors[t] * row
            row = tiles[home][line : line + 1, :] * jnp.concatenate([scale] * (width // LANES), axis=1)
            for t in range(low, count):
                wide = jnp.concatenate([factors[t]] * (width // LANES), axis=1)
                tiles[t] = tiles[t] - wide * row
    return tiles


def factor_gram(read_rows, size, work_ref, with_inverse=False):
    for first in range(0, size, PANEL):
        rows = pl.ds(first, PANEL)
        begin, end = first // LANES * LANES, size
        block = read_rows(first)[:, begin:]
        row_ids = lax.broadcasted_iota(jnp.int32, (PANEL, size), 0) + first
        column_ids = lax.broadcasted_iota(jnp.int32, (PANEL, size), 1)
        if with_inverse:
            reach = -(-(first + PANEL) // LANES) * LANES
            end = size + reach
            unit = (row_ids == column_ids).astype(jnp.float32)
            block = jnp.concatenate([block, unit[:, :reach]], axis=1)
        if first:
            block = block - product(
                work_ref[0:first, first : first + PANEL], work_ref[0:first, begin:end], (0, 0)
            )
        tiles = [block[t : t + TILE, :] for t in range(0, PANEL, TILE)]
        block = jnp.concatenate(eliminate(tiles, first - begin), axis=0)
        square = block[:, : size - begin]
        ahead = column_ids[:, begin:] - row_ids[:, begin:]
        pivots = jnp.sum(jnp.where(ahead == 0, square, 0.0), axis=1, keepdims=True)
        scale = lax.rsqrt(pivots)
        work_ref[rows, begin:size] = jnp.where(ahead >= 0, square * scale, 0.0)
        if begin:
            work_ref[rows, 0:begin] = jnp.zeros((PANEL, begin), jnp.float32)
        if with_inverse:
            work_ref[rows, size:end] = block[:, size - begin :] * scale
            if end < 2 * size:
                work_ref[rows, end:] = jnp.zeros((PANEL, 2 * size - end), jnp.float32)


def mix_tensor(left, tensor_ref, out_ref):
    count, size, _ = tensor_ref.shape
    for p in range(count):
        mixed = product(left, tensor_ref[p], (1, 0))
        for block in range(size // TILE):
            for half in range(size // LANES):
                out_ref[block, pl.ds(half * TILE * count + p, TILE, stride=count), :] = mixed[
                    block * TILE : (block + 1) * TILE, half * LANES : (half + 1) * LANES
                ]


def child_matrix(leaf_ref, gathered_ref, side, out_ref):
    size = out_ref.shape[0]

    def read_rows(first):
        members = pl.ds(first // TILE, PANEL // TILE)
        return gathered_ref[members, side].reshape(PANEL, size)

    @pl.when(leaf_ref[0] > 0)
    def _():
        out_ref[...] = gathered_ref[:, side].reshape(size, size)

    @pl.when(leaf_ref[0] == 0)
    def _():
        factor_gram(read_rows, size, out_ref)


def mix_left_kernel(leaf_ref, gathered_ref, tensor_hbm, out_hbm, tensor_ref, left_ref, mixed_ref, load_sem, store_sems):
    load = pltpu.make_async_copy(tensor_hbm, tensor_ref, load_sem)
    load.start()
    child_matrix(leaf_ref, gathered_ref, 0, left_ref)
    load.wait()
    mix_tensor(left_ref[...], tensor_ref, mixed_ref)
    pieces = store_sems.shape[0]
    length = mixed_ref.shape[0] // pieces
    stores = []
    for i in range(pieces):
        part = pl.ds(i * length, length)
        stores.append(pltpu.make_async_copy(mixed_ref.at[part], out_hbm.at[part], store_sems.at[i]))
    for store in stores:
        store.start()
    for store in stores:
        store.wait()


def mix_left(leaf, gathered, tensor):
    count, size, _ = tensor.shape
    shape = (size // TILE, size // LANES * TILE * count, LANES)
    mixed = pl.pallas_call(
        mix_left_kernel,
        in_specs=[
            pl.BlockSpec(memory_space=pltpu.SMEM),
            pl.BlockSpec(memory_space=VMEM),
            pl.BlockSpec(memory_space=pl.ANY),
        ],
        out_specs=pl.BlockSpec(memory_space=pltpu.HBM),
        out_shape=jax.ShapeDtypeStruct(shape, jnp.float32),
        scratch_shapes=[
            VMEM(tensor.shape, jnp.float32),
            VMEM((size, size), jnp.float32),
            VMEM(shape, jnp.float32),
            pltpu.SemaphoreType.DMA(()),
            pltpu.SemaphoreType.DMA((4,)),
        ],
        compiler_params=pltpu.CompilerParams(vmem_limit_bytes=61_000_000),
        name="mix_left",
    )(leaf, gathered, tensor)
    return lax.all_to_all(mixed, "cuts", 0, 0, tiled=True)


def right_factor_kernel(leaf_ref, gathered_ref, out_ref):
    child_matrix(leaf_ref, gathered_ref, 1, out_ref)


def right_factor(leaf, gathered):
    size = gathered.shape[-1]
    return pl.pallas_call(
        right_factor_kernel,
        in_specs=[
            pl.BlockSpec(memory_space=pltpu.SMEM),
            pl.BlockSpec(memory_space=VMEM),
        ],
        out_shape=jax.ShapeDtypeStruct((size, size), jnp.float32),
        cost_estimate=pl.CostEstimate(
            flops=8 * 10**9, bytes_accessed=3 * 4 * size * size, transcendentals=size
        ),
        compiler_params=PARAMS,
        name="right_factor",
    )(leaf, gathered)


def mix_right_kernel(right_ref, halfway_ref, mixed_hbm, gram_ref, mixed_ref, store_sems):
    size = gram_ref.shape[0]
    right = right_ref[...]
    lines = mixed_ref.shape[0]
    parents = halfway_ref.shape[1] // (lines * (size // LANES))
    stores = []
    for x in range(lines):
        halves = []
        for half in range(size // LANES):
            rows = pl.ds((half * lines + x) * parents, parents)
            halves.append(halfway_ref[:, rows, :].reshape(size, LANES))
        mixed = product(jnp.concatenate(halves, axis=1), right, (1, 1))
        mixed_ref[x] = mixed
        stores.append(pltpu.make_async_copy(mixed_ref.at[x], mixed_hbm.at[x], store_sems.at[x]))
        stores[x].start()
        term = product(mixed, mixed, (1, 1))
        gram_ref[...] = term if x == 0 else gram_ref[...] + term
    for store in stores:
        store.wait()


def mix_right(halfway, right):
    size = right.shape[-1]
    mixed, partial = pl.pallas_call(
        mix_right_kernel,
        out_specs=[
            pl.BlockSpec(memory_space=pltpu.HBM),
            pl.BlockSpec(memory_space=VMEM),
        ],
        out_shape=[
            jax.ShapeDtypeStruct((TILE, size, size), jnp.float32),
            jax.ShapeDtypeStruct((size, size), jnp.float32),
        ],
        scratch_shapes=[
            VMEM((TILE, size, size), jnp.float32),
            pltpu.SemaphoreType.DMA((TILE,)),
        ],
        compiler_params=PARAMS,
        name="mix_right",
    )(right, halfway)
    cut_count = lax.axis_size("cuts")
    pieces = lax.all_to_all(
        partial.reshape(cut_count, size // cut_count, size), "cuts", 0, 0, tiled=True
    )
    return mixed, jnp.sum(pieces, axis=0)


def last_kernel(place_ref, gathered_ref, mixed_hbm, basis_ref, upper_ref, mixed_ref, work_ref, wide_ref, done):
    size = mixed_ref.shape[1]
    lines = mixed_ref.shape[0]
    copy = pltpu.make_async_copy(mixed_hbm, mixed_ref, done)
    copy.start()

    def read_rows(first):
        members = pl.ds(first // TILE, PANEL // TILE)
        return gathered_ref[members].reshape(PANEL, size)

    factor_gram(read_rows, size, work_ref, with_inverse=True)
    active = place_ref[1] > 0
    mine = pl.ds(pl.multiple_of(place_ref[0] * TILE, TILE), TILE)
    upper_ref[...] = jnp.where(active, work_ref[mine, 0:size], 0.0)
    copy.wait()

    @pl.when(active)
    def _():
        inverse = work_ref[:, size:] * size
        for x in range(lines):
            solved = product(inverse, mixed_ref[x], (1, 0))
            for half in range(size // LANES):
                wide_ref[half, pl.ds(x, size, stride=lines), :] = solved[:, half * LANES : (half + 1) * LANES]
        for half in range(size // LANES):
            columns = pl.ds(half * LANES, LANES)
            basis_ref[:, :, columns] = wide_ref[half].reshape(size, lines, LANES)

    @pl.when(jnp.logical_not(active))
    def _():
        basis_ref[...] = jnp.zeros_like(basis_ref)


def last(place, gathered, mixed):
    lines, size, _ = mixed.shape
    whole = pl.BlockSpec(memory_space=VMEM)
    return pl.pallas_call(
        last_kernel,
        in_specs=[
            pl.BlockSpec(memory_space=pltpu.SMEM),
            whole,
            pl.BlockSpec(memory_space=pl.ANY),
        ],
        out_specs=[whole, whole],
        out_shape=[
            jax.ShapeDtypeStruct((size, lines, size), jnp.float32),
            jax.ShapeDtypeStruct((TILE, size), jnp.float32),
        ],
        scratch_shapes=[
            VMEM(mixed.shape, jnp.float32),
            VMEM((size, 2 * size), jnp.float32),
            VMEM((size // LANES, size * lines, LANES), jnp.float32),
            pltpu.SemaphoreType.DMA(()),
        ],
        compiler_params=PARAMS,
        name="last",
    )(place, gathered, mixed)


def unwritten(shape):
    return pl.pallas_call(
        lambda out_ref: None,
        out_specs=pl.BlockSpec(memory_space=pltpu.HBM),
        out_shape=jax.ShapeDtypeStruct(shape, jnp.float32),
        compiler_params=PARAMS,
        name="unwritten",
    )()


def pick_children(rows_here, held, children):
    chosen, rows_here = lax.optimization_barrier(
        ([held == child for child in children], rows_here)
    )
    table = from_everyone(rows_here, "node")
    picked = [jnp.sum(jnp.where(mask[:, None, None], table, 0.0), axis=0) for mask in chosen]
    return jnp.stack(picked)


def shards(transfer, leaf_factors, node_of_slot):
    slot_count = lax.axis_size("node")
    group_index = lax.axis_index("node")
    member_index = lax.axis_index("cuts")
    tensor = transfer[0]
    slot_ids = lax.iota(jnp.int32, slot_count)
    node_id = jnp.sum(jnp.where(slot_ids == group_index, node_of_slot, 0))
    log_slots = slot_count.bit_length() - 1
    my_depth = jnp.zeros((), jnp.int32)
    for level_bit in range(1, log_slots):
        my_depth = my_depth + (node_id >= 2**level_bit).astype(jnp.int32)
    children = [(2 * node_id + side) % slot_count for side in range(2)]
    place = jnp.stack([member_index.astype(jnp.int32), my_depth])

    def process(leaf, rows, mixed, rows_here):
        gathered = from_everyone(rows, "cuts")
        halfway = mix_left(leaf, gathered, tensor)
        return mix_right(halfway, right_factor(leaf, gathered))

    def keep(leaf, rows, mixed, rows_here):
        return mixed, rows_here

    def pick_inner(rows, rows_here):
        return pick_children(rows_here, node_of_slot, children)

    def level(step, state):
        rows, mixed, rows_here = state
        leaf = (step == 0).astype(jnp.int32).reshape(1)
        mixed, rows_here = lax.cond(
            my_depth == log_slots - 1 - step, process, keep, leaf, rows, mixed, rows_here
        )
        more = step < log_slots - 2
        rows = lax.cond(more, pick_inner, lambda rows, rows_here: rows, rows, rows_here)
        return rows, mixed, rows_here

    leaf_table = from_everyone(leaf_factors[0], "node")
    masks = [(slot_ids == child)[:, None, None] for child in children]
    rows = jnp.stack([jnp.sum(jnp.where(mask, leaf_table, 0.0), axis=0) for mask in masks])
    state = (rows, unwritten(tensor.shape), leaf_factors[0])
    _, mixed, rows_here = lax.fori_loop(0, log_slots - 1, level, state)
    place, rows_here = lax.optimization_barrier((place, rows_here))

    gathered = from_everyone(rows_here, "cuts")
    basis, upper = last(place, gathered, mixed)
    return basis[None], upper[None]


def solution(mesh):
    placed = (P("node", "cuts", None, None), P("node", "cuts", None), P())
    return jax.shard_map(
        shards,
        mesh=mesh,
        in_specs=placed,
        out_specs=(P("node", None, "cuts", None), P("node", "cuts", None)),
        check_vma=False,
    )
```
